32 devices in a mesh: dp: 16 (over z, x, core), tensor: 2 (over y).
Axes of the slice: x: 2, y: 2, z: 4, core: 2. Of those that a mesh axis runs over, the one named last changes fastest.
Arguments:
- inputs: bfloat16 [2048, 2048], P('dp'), may hold values from -6 to 6
- segments: int32 [2048], P('dp'), may hold values from 0 to 1, as said below
- positions: int32 [2048], P('dp'), may hold values from 0 to 1999, as said below
- w_query: bfloat16 [2048, 2048], P('dp', 'tensor')
- w_key: bfloat16 [2048, 512], P('dp', 'tensor')
- w_value: bfloat16 [2048, 512], P('dp', 'tensor'), may hold values from -0.125 to 0.125
- w_out: bfloat16 [2048, 2048], P('dp', 'tensor'), may hold values from -0.5 to 0.5
- w_gate: bfloat16 [2048, 8192], P('dp', 'tensor'), may hold values from -0.125 to 0.125
- w_up: bfloat16 [2048, 8192], P('dp', 'tensor'), may hold values from -0.125 to 0.125
- w_down: bfloat16 [2048, 8192], P('dp', 'tensor'), may hold values from -0.125 to 0.125
- attn_gain: bfloat16 [2048], P('dp'), may hold values from 0.5 to 1.5
- mlp_gain: bfloat16 [2048], P('dp'), may hold values from 0.5 to 1.5
- out_grad: bfloat16 [2048, 2048], P('dp'), may hold values from -6 to 6
Outputs:
- output: bfloat16 [2048, 2048], P('dp')
- input_grad: float32 [2048, 2048], P('dp')
- query_grad: float32 [2048, 2048], P('dp', 'tensor')
- key_grad: float32 [2048, 512], P('dp', 'tensor')
- value_grad: float32 [2048, 512], P('dp', 'tensor')
- out_proj_grad: float32 [2048, 2048], P('dp', 'tensor')
- gate_grad: float32 [2048, 8192], P('dp', 'tensor')
- up_grad: float32 [2048, 8192], P('dp', 'tensor')
- down_grad: float32 [2048, 8192], P('dp', 'tensor')
- attn_gain_grad: float32 [2048], P('dp')
- mlp_gain_grad: float32 [2048], P('dp')
The draws below stay inside these ranges and needn't reach their ends.
Inputs may be any that keep to these rules, and one draw needn't show every extreme that they name: `segments`: within each sequence of 128 tokens segment numbers start at 0 and rise by one where a document begins; documents span 200 to 2000 tokens of the packed stream, so a sequence's first document may have begun in the sequence before it. `positions`: A token's position within its document: it rises by one from token to token of a document and is 0 where a document begins; at a sequence's first token it continues a document that began earlier.
All inputs are finite; a program needn't handle non-finite values.
Results may differ from the reference program's by a relative error of at most 0.019.
The reference program's roundings to bfloat16 on the way count: a program that leaves them out, or rounds other values in their place, can miss the bound.
Values may be sent and summed in bfloat16 or wider, within the bound.
No kernel may reach another device: no remote copies, remote signals or barrier semaphores. Data moves between devices by JAX's collectives and lax.ppermute only.
A program may use at most 256 MiB of HBM per device.

```python
import math
import jax
import jax.numpy as jnp
from jax import lax

D = 2048
HEADS = 32
KV_HEADS = 8
HEAD_DIM = 64
FF = 8192
TOK_DEV = 128
DOC_MIN = 200
DOC_MAX = 2000
TOKENS = 2048


def doc_layout(key):
    count = TOKENS // TOK_DEV
    lengths = jax.random.randint(jax.random.fold_in(key, 7), (count, 8), DOC_MIN, DOC_MAX + 1)
    lengths = lengths.at[0, 0].set(DOC_MAX)
    lengths = lengths.at[1, 1:].set(DOC_MIN)
    offset = jax.random.randint(jax.random.fold_in(key, 11), (count,), 0, lengths[:, 0])
    offset = offset.at[0].set(DOC_MAX - TOK_DEV)
    offset = offset.at[1].set(lengths[1, 0] - 1)
    ends = jnp.cumsum(lengths, axis=1) - offset[:, None]
    starts = ends - lengths
    index = jnp.arange(TOK_DEV, dtype=jnp.int32)
    segment = jnp.sum((ends[:, None, :] <= index[None, :, None]).astype(jnp.int32), axis=2)
    start_of = jnp.take_along_axis(starts, segment, axis=1)
    position = index[None, :] - start_of
    return (segment.reshape(-1).astype(jnp.int32), position.reshape(-1).astype(jnp.int32))


def draw_segments(key, part):
    return doc_layout(key)[0]


def draw_positions(key, part):
    return doc_layout(key)[1]


def draw_w_query(key, part):
    values = jax.random.normal(key, (D, HEADS * HEAD_DIM), jnp.float32) * D ** (-0.5)
    return values.astype(jnp.bfloat16)


def draw_w_key(key, part):
    values = jax.random.normal(key, (D, KV_HEADS * HEAD_DIM), jnp.float32) * D ** (-0.5)
    return values.astype(jnp.bfloat16)


def raised(drawn, rng, source, target, parts, factor):
    owner, partner = [(jnp.arange(drawn.shape[axis_at]) // (drawn.shape[axis_at] // parts)).reshape([-1 if axis == axis_at else 1 for axis in range(drawn.ndim)]) for axis_at in (source, target)]
    chosen = jax.random.permutation(rng, parts)[partner]
    strong = (owner == chosen) | (owner == (partner + parts // 2) % parts)
    return jnp.where(strong, factor * drawn, drawn)


def steps_of(stream_key, shape, split, low, high):
    def one(dim, shards_of):
        draws = jax.random.uniform(jax.random.fold_in(jax.random.fold_in(stream_key, 6), dim), (shards_of,), jnp.float32, low / len(split), high / len(split))
        return jnp.repeat(jnp.exp(draws), shape[dim] // shards_of).reshape((-1,) + (1,) * (len(shape) - dim - 1))

    factor_of = one(*split[0])
    for cut in split[1:]:
        factor_of = factor_of * one(*cut)
    return factor_of


def normal_values(own_key, shape, spread, bound, shards=(), kind=jnp.bfloat16):
    level = steps_of(own_key, shape, shards, -0.22, 0.18) if shards else 1.0
    values = jax.random.normal(own_key, shape, jnp.float32) * spread * level
    return jnp.minimum(jnp.maximum(values, -bound), bound).astype(kind)


def noise_with(key, dims, width, limit, pieces, heavy, kind=jnp.bfloat16):
    array = width * jax.random.normal(key, dims, jnp.float32)
    if pieces:
        array = array * steps_of(key, dims, pieces, -0.22, 0.18)
    return jnp.clip(raised(array, jax.random.fold_in(key, 3), *heavy), -limit, limit).astype(kind)


def setup_inputs(seed: int = 0) -> dict:
    key_of = jax.random.split(jax.random.key(seed), 14)
    return {
        "inputs": normal_values(key_of[0], (TOKENS, D), 1.0, 6.0, ((0, 16),)),
        "segments": draw_segments(jax.random.fold_in(key_of[13], 71), 0),
        "positions": draw_positions(jax.random.fold_in(key_of[13], 71), 0),
        "w_query": draw_w_query(jax.random.fold_in(key_of[13], 71), 0),
        "w_key": draw_w_key(jax.random.fold_in(key_of[13], 71), 0),
        "w_value": normal_values(key_of[5], (D, KV_HEADS * HEAD_DIM), D ** -0.5, 0.125, ((0, 16), (1, 2))),
        "w_out": normal_values(key_of[6], (D, HEADS * HEAD_DIM), (HEADS * HEAD_DIM // 16) ** -0.5, 0.5, ((0, 16), (1, 2))),
        "w_gate": normal_values(key_of[7], (D, FF), D ** -0.5, 0.125, ((0, 16), (1, 2))),
        "w_up": normal_values(key_of[8], (D, FF), D ** -0.5, 0.125, ((0, 16), (1, 2))),
        "w_down": normal_values(key_of[9], (D, FF), (FF // 4) ** -0.5, 0.125, ((0, 16), (1, 2))),
        "attn_gain": jnp.clip(1.0 + 0.1 * jax.random.normal(key_of[10], (D,), jnp.float32), 0.5, 1.5).astype(jnp.bfloat16),
        "mlp_gain": jnp.clip(1.0 + 0.1 * jax.random.normal(key_of[11], (D,), jnp.float32), 0.5, 1.5).astype(jnp.bfloat16),
        "out_grad": noise_with(key_of[12], (TOKENS, D), 1.0, 6.0, ((0, 16),), (0, 1, 16, 2.0)),
    }


norm_eps = 1e-05
rope_base = 500000.0
masked_score = -1e+30

@jax.custom_vjp
def low(v):
    return lax.optimization_barrier(v.astype(jnp.bfloat16)).astype(jnp.float32)

@jax.custom_vjp
def low_back(v):
    return v

def low_keep(v):
    return (low(v), None)

def low_pass(kept, grad):
    return (grad,)

def back_keep(v):
    return (v, None)

def back_low(kept, grad):
    return (low(grad),)
low.defvjp(low_keep, low_pass)
low_back.defvjp(back_keep, back_low)

def rope_freqs(head_dim):
    index = jnp.arange(head_dim // 2, dtype=jnp.float32)
    inverse = rope_base ** (-2.0 * index / head_dim)
    wavelen = 2.0 * math.pi / inverse
    smooth = (8192.0 / wavelen - 1.0) / 3.0
    scaled = (1.0 - smooth) * inverse / 32.0 + smooth * inverse
    return jnp.where(wavelen < 2048.0, inverse, jnp.where(wavelen > 8192.0, inverse / 32.0, scaled))

def rotate(values, cosine, sine):
    half = values.shape[-1] // 2
    first = values[..., :half]
    second = values[..., half:]
    return jnp.concatenate([first * cosine - second * sine, second * cosine + first * sine], axis=-1)

def rms_norm(values, gain):
    scale = lax.rsqrt(lax.optimization_barrier(jnp.mean(values * values, axis=-1, keepdims=True)) + norm_eps)
    return values * scale * gain

def matmul(left, right):
    return jnp.dot(left, right, precision=lax.Precision.HIGHEST)

def attend(items):
    query, key_rot, value, segment = items
    factor = query.shape[-1] ** (-0.5)
    scores = jnp.einsum('qhgd,khd->hgqk', query, key_rot, precision=lax.Precision.HIGHEST) * factor
    scores = low_back(scores)
    order = jnp.arange(segment.shape[0])
    allowed = (segment[:, None] == segment[None, :]) & (order[:, None] >= order[None, :])
    scores = jnp.where(allowed, scores, masked_score)
    probs = low(jax.nn.softmax(scores, axis=-1))
    return jnp.einsum('hgqk,khd->qhgd', probs, value, precision=lax.Precision.HIGHEST)

def forward(inputs, w_query, w_key, w_value, w_out, w_gate, w_up, w_down, attn_gain, mlp_gain, cosine, sine, segments):
    count = TOKENS // TOK_DEV
    group = HEADS // KV_HEADS
    normed = low(rms_norm(inputs, attn_gain))
    query = low(rotate(low_back(matmul(normed, w_query)).reshape(TOKENS, HEADS, HEAD_DIM), cosine, sine))
    key_rot = low(rotate(low_back(matmul(normed, w_key)).reshape(TOKENS, KV_HEADS, HEAD_DIM), cosine, sine))
    value = low(low_back(matmul(normed, w_value)))
    attended = lax.map(jax.checkpoint(attend), (query.reshape(count, TOK_DEV, KV_HEADS, group, HEAD_DIM), key_rot.reshape(count, TOK_DEV, KV_HEADS, HEAD_DIM), value.reshape(count, TOK_DEV, KV_HEADS, HEAD_DIM), segments.reshape(count, TOK_DEV)))
    attended = low(low_back(attended.reshape(TOKENS, HEADS * HEAD_DIM)))
    middle = inputs + low_back(matmul(attended, w_out.T))
    normed_two = low(rms_norm(middle, mlp_gain))
    gate = low_back(matmul(normed_two, w_gate))
    upward = low_back(matmul(normed_two, w_up))
    active = low(jax.nn.silu(gate) * upward)
    return middle + low_back(matmul(active, w_down.T))

def reference(inputs, segments, positions, w_query, w_key, w_value, w_out, w_gate, w_up, w_down, attn_gain, mlp_gain, out_grad):
    angle = positions.astype(jnp.float32)[:, None] * rope_freqs(HEAD_DIM)[None, :]
    cosine = jnp.cos(angle)[:, None, :]
    sine = jnp.sin(angle)[:, None, :]
    floats = [a.astype(jnp.float32) for a in (inputs, w_query, w_key, w_value, w_out, w_gate, w_up, w_down, attn_gain, mlp_gain)]

    def apply(*values):
        return forward(*values, cosine, sine, segments)
    result, pullback = jax.vjp(apply, *floats)
    grads = pullback(out_grad.astype(jnp.float32))
    return (result.astype(jnp.bfloat16), grads[0], grads[1], grads[2], grads[3], grads[4], grads[5], grads[6], grads[7], grads[8], grads[9])
```

```python
import math

import jax
import jax.numpy as jnp
from jax import lax
from jax.sharding import PartitionSpec as P

HEADS = 32
KV_HEADS = 8
HEAD_DIM = 64
PLANES = 4

norm_eps = 1e-05
rope_base = 500000.0
masked_score = -1e30

f32 = jnp.float32
bf16 = jnp.bfloat16


def rope_freqs(head_dim):
    index = jnp.arange(head_dim // 2, dtype=f32)
    inverse = rope_base ** (-2.0 * index / head_dim)
    wavelen = 2.0 * math.pi / inverse
    smooth = (8192.0 / wavelen - 1.0) / 3.0
    scaled = (1.0 - smooth) * inverse / 32.0 + smooth * inverse
    return jnp.where(wavelen < 2048.0, inverse, jnp.where(wavelen > 8192.0, inverse / 32.0, scaled))


def rotate(values, cosine, sine):
    half = values.shape[-1] // 2
    first = values[..., :half]
    second = values[..., half:]
    return jnp.concatenate(
        [first * cosine - second * sine, second * cosine + first * sine], axis=-1
    )


def norm_parts(values):
    scale = lax.rsqrt(jnp.mean(values * values, axis=-1, keepdims=True) + norm_eps)
    return (values * scale, scale)


def norm_back(grad, unit, scale, gain):
    weighted = grad * gain
    return scale * (weighted - unit * jnp.mean(weighted * unit, axis=-1, keepdims=True))


def dot(left, right):
    return jnp.dot(left, right, preferred_element_type=f32)


def dot_last(left, right):
    return lax.dot_general(left, right, (((1,), (1,)), ((), ())), preferred_element_type=f32)


def dot_first(left, right):
    return lax.dot_general(left, right, (((0,), (0,)), ((), ())), preferred_element_type=f32)


class Layout:
    def __init__(self, count):
        self.count = count
        self.inner = count // PLANES
        self.bits = self.inner.bit_length() - 1
        self.rel = []
        for place in range(count):
            plane, rest = place % PLANES, place // PLANES
            inner = sum(((rest >> (self.bits - 1 - b)) & 1) << b for b in range(self.bits))
            self.rel.append(plane * self.inner + inner)
        self.place = {r: p for p, r in enumerate(self.rel)}
        self.me = lax.axis_index("dp")
        self.side = lax.axis_index("tensor")
        self.plane = self.me // self.inner

    def swap(self, array, mask):
        return lax.ppermute(array, "dp", [(i, i ^ mask) for i in range(self.count)])

    def swap_plane(self, array, j):
        return self.swap(array, j * self.inner)

    def swap_side(self, array):
        return lax.ppermute(array, "tensor", [(0, 1), (1, 0)])

    def own_order(self, array):
        rows, width = array.shape[0], array.shape[1] // self.count
        return jnp.concatenate(
            [lax.dynamic_slice(array, (0, (self.me ^ r) * width), (rows, width)) for r in self.rel], axis=1
        )

    def true_order(self, array):
        rows, width = array.shape[0], array.shape[1] // self.count
        mine = sum(((self.me >> b) & 1) * self.place[1 << b] for b in range(self.count.bit_length() - 1))
        return jnp.concatenate(
            [
                lax.dynamic_slice(array, (0, (mine ^ self.place[a]) * width), (rows, width))
                for a in range(self.count)
            ],
            axis=1,
        )

    def other_plane_order(self, array, j):
        width = array.shape[1] // self.count
        places = [p ^ j for p in range(self.count)]
        return jnp.concatenate([array[:, p * width : (p + 1) * width] for p in places], axis=1)

    def half(self, array, other=False):
        size = array.shape[0] // 2
        side = 1 - self.side if other else self.side
        return lax.dynamic_slice_in_dim(array, side * size, size, 0)

    def join_sides(self, mine, other):
        return jnp.where(
            self.side == 0, jnp.concatenate([mine, other], 0), jnp.concatenate([other, mine], 0)
        )

    def grow(self, rows):
        for b in reversed(range(self.bits)):
            rows = jnp.concatenate([rows, self.swap(rows, 1 << b)], axis=0)
        return rows

    def gather_rows(self, rows):
        planes = [rows] + [self.swap_plane(rows, j) for j in range(1, PLANES)]
        return self.grow(jnp.concatenate(planes, axis=0))

    def gather_column_block(self, weights):
        def block(j):
            size = weights[0].shape[1] // PLANES
            return jnp.concatenate(
                [lax.dynamic_slice_in_dim(w, (self.plane ^ j) * size, size, 1) for w in weights], axis=1
            )

        planes = [block(0)] + [self.swap_plane(block(j), j) for j in range(1, PLANES)]
        return self.grow(jnp.concatenate(planes, axis=0))

    def shrink(self, partial, dtypes):
        for b in range(self.bits):
            size = partial.shape[0] // 2
            sent = partial[size:].astype(dtypes[min(b, len(dtypes) - 1)])
            partial = partial[:size] + self.swap(sent, 1 << b).astype(f32)
        return partial

    def scatter_rows(self, partial, dtypes):
        partial = self.shrink(partial, dtypes)
        size = partial.shape[0] // PLANES
        total = partial[:size]
        for j in range(1, PLANES):
            sent = partial[j * size : (j + 1) * size].astype(dtypes[-1])
            total = total + self.swap_plane(sent, j).astype(f32)
        return total

    def scatter_column_block(self, partial, dtypes, parts):
        partial = self.shrink(partial, dtypes)
        size = partial.shape[0] // PLANES
        width = partial.shape[1] // parts
        pieces = [partial[:size]]
        for j in range(1, PLANES):
            sent = partial[j * size : (j + 1) * size].astype(dtypes[-1])
            pieces.append(self.swap_plane(sent, j).astype(f32))
        outs = []
        for part in range(parts):
            out = jnp.zeros((size, width * PLANES), f32)
            for j in range(PLANES):
                piece = pieces[j][:, part * width : (part + 1) * width]
                out = lax.dynamic_update_slice(out, piece, (0, (self.plane ^ j) * width))
            outs.append(out)
        return outs

    def gather_tokens(self, rows):
        planes = [rows]
        for j in range(1, PLANES):
            planes.append(self.other_plane_order(self.swap_plane(rows, j), j))
        rows = jnp.concatenate(planes, axis=0)
        return jnp.concatenate([rows, self.swap_side(rows)], axis=0)

    def scatter_tokens(self, partial, dtype):
        size = partial.shape[0] // 2
        partial = partial[:size] + self.swap_side(partial[size:].astype(dtype)).astype(f32)
        size = size // PLANES
        total = partial[:size]
        for j in range(1, PLANES):
            sent = self.other_plane_order(partial[j * size : (j + 1) * size].astype(dtype), j)
            total = total + self.swap_plane(sent, j).astype(f32)
        return total

    def scatter_features(self, vector):
        for b in range(self.bits):
            size = vector.shape[1] // 2
            vector = vector[:, :size] + self.swap(vector[:, size:], 1 << b)
        size = vector.shape[1] // PLANES
        total = vector[:, :size]
        for j in range(1, PLANES):
            total = total + self.swap_plane(vector[:, j * size : (j + 1) * size], j)
        return total + self.swap_side(total)


def on_device(
    inputs,
    segments,
    positions,
    w_query,
    w_key,
    w_value,
    w_out,
    w_gate,
    w_up,
    w_down,
    attn_gain,
    mlp_gain,
    out_grad,
):
    lay = Layout(lax.axis_size("dp"))
    length = inputs.shape[0]
    group = HEADS // KV_HEADS
    factor = HEAD_DIM ** (-0.5)
    q_cols, kv_cols = w_query.shape[1], w_key.shape[1]
    qkv_cols = q_cols + 2 * kv_cols

    gains = jnp.pad(jnp.stack([attn_gain, mlp_gain], axis=1), ((0, 0), (0, 126)))
    qkv_full = lay.gather_rows(jnp.concatenate([w_query, w_key, w_value, gains], axis=1))
    out_full = lay.gather_rows(w_out)
    gains = qkv_full[:, qkv_cols : qkv_cols + 2].T.astype(f32)
    gain_one, gain_two = gains[0:1], gains[1:2]
    qkv_full = qkv_full[:, :qkv_cols]
    gate_up = lay.gather_column_block([w_gate, w_up])
    down = lay.gather_column_block([w_down])
    hidden = down.shape[1]

    residual = lay.own_order(inputs).astype(f32)
    grad_own = lay.own_order(out_grad)
    grad_half = lay.half(grad_own)
    grad_all = lay.gather_tokens(grad_half)
    angle = positions.astype(f32)[:, None] * rope_freqs(HEAD_DIM)[None, :]
    cosine = jnp.cos(angle)[:, None, :]
    sine = jnp.sin(angle)[:, None, :]
    order = jnp.arange(length)
    allowed = (segments[:, None] == segments[None, :]) & (order[:, None] >= order[None, :])
    unit_one, scale_one = norm_parts(residual)
    normed_one = (unit_one * gain_one).astype(bf16)
    qkv = dot(normed_one, qkv_full)
    query_rot = rotate(qkv[:, :q_cols].reshape(length, -1, HEAD_DIM), cosine, sine).astype(bf16)
    key_rot = rotate(
        qkv[:, q_cols : q_cols + kv_cols].reshape(length, -1, HEAD_DIM), cosine, sine
    ).astype(bf16)
    value_heads = qkv[:, q_cols + kv_cols :].astype(bf16).reshape(length, -1, HEAD_DIM)
    kv_local = key_rot.shape[1]
    query_group = query_rot.reshape(length, kv_local, group, HEAD_DIM)
    scores = jnp.where(
        allowed,
        jnp.einsum("qhgd,khd->hgqk", query_group, key_rot, preferred_element_type=f32) * factor,
        masked_score,
    )
    top = jnp.max(scores, axis=-1, keepdims=True)
    expo = jnp.exp(scores - top)
    total = jnp.sum(expo, axis=-1, keepdims=True)
    probs = expo / total
    weights_low = probs.astype(bf16)
    attended = (
        jnp.einsum("hgqk,khd->qhgd", weights_low, value_heads, preferred_element_type=f32)
        .astype(bf16)
        .reshape(length, -1)
    )
    share = dot_last(attended, out_full)
    middle = (
        lay.half(residual) + lay.half(share) + lay.swap_side(lay.half(share, other=True))
    )

    unit_two, scale_two = norm_parts(middle)
    normed_two = lay.gather_tokens((unit_two * gain_two).astype(bf16))
    gate_and_up = dot(normed_two, gate_up)
    gate, upward = gate_and_up[:, :hidden], gate_and_up[:, hidden:]
    sigma = jax.nn.sigmoid(gate)
    active = (gate * sigma * upward).astype(bf16)
    mlp_out = lay.scatter_tokens(dot_last(active, down), bf16)
    output = (middle + mlp_out).astype(bf16)
    output = lay.true_order(lay.join_sides(output, lay.swap_side(output)))

    active_grad = dot(grad_all, down)
    gate_delta = (active_grad * upward * sigma * (1.0 + gate * (1.0 - sigma))).astype(bf16)
    up_delta = (active_grad * gate * sigma).astype(bf16)
    both_delta = jnp.concatenate([gate_delta, up_delta], axis=1)
    normed_two_grad = lay.scatter_tokens(dot_last(both_delta, gate_up), f32)
    (down_grad,) = lay.scatter_column_block(dot_first(grad_all, active), (f32, bf16), 1)
    gate_grad, up_grad = lay.scatter_column_block(dot_first(normed_two, both_delta), (f32, bf16), 2)
    middle_grad = grad_half.astype(f32) + norm_back(normed_two_grad, unit_two, scale_two, gain_two)
    mlp_gain_part = jnp.sum(normed_two_grad * unit_two, axis=0, keepdims=True)

    attn_delta = middle_grad.astype(bf16)
    attn_delta = lay.join_sides(attn_delta, lay.swap_side(attn_delta))
    middle_grad = lay.join_sides(middle_grad, lay.swap_side(middle_grad))
    out_proj_grad = lay.scatter_rows(dot_first(attn_delta, attended), (f32, bf16))
    head_delta = (
        dot(attn_delta, out_full).astype(bf16).reshape(length, kv_local, group, HEAD_DIM)
    )
    prob_grad = jnp.einsum("qhgd,khd->hgqk", head_delta, value_heads, preferred_element_type=f32)
    row_total = jnp.sum(probs * prob_grad, axis=-1, keepdims=True)
    score_delta = (probs * (prob_grad - row_total)).astype(bf16)
    query_rot_grad = (
        jnp.einsum("hgqk,khd->qhgd", score_delta, key_rot, preferred_element_type=f32) * factor
    )
    key_rot_grad = (
        jnp.einsum("hgqk,qhgd->khd", score_delta, query_group, preferred_element_type=f32) * factor
    )
    value_delta = (
        jnp.einsum("hgqk,qhgd->khd", weights_low, head_delta, preferred_element_type=f32)
        .astype(bf16)
        .reshape(length, -1)
    )
    query_delta = (
        rotate(query_rot_grad.reshape(length, -1, HEAD_DIM), cosine, -sine)
        .astype(bf16)
        .reshape(length, -1)
    )
    key_delta = rotate(key_rot_grad, cosine, -sine).astype(bf16).reshape(length, -1)
    qkv_delta = jnp.concatenate([query_delta, key_delta, value_delta], axis=1)
    share = dot_last(qkv_delta, qkv_full)
    normed_one_grad = share + lay.swap_side(share.astype(bf16)).astype(f32)
    attn_gain_part = jnp.sum(share * unit_one, axis=0, keepdims=True)
    input_grad = middle_grad + norm_back(normed_one_grad, unit_one, scale_one, gain_one)
    input_grad = lay.true_order(input_grad)
    qkv_grad = lay.scatter_rows(dot_first(normed_one, qkv_delta), (f32, bf16))
    gain_grads = lay.scatter_features(jnp.concatenate([attn_gain_part, mlp_gain_part], axis=0))
    return (
        output,
        input_grad,
        qkv_grad[:, :q_cols],
        qkv_grad[:, q_cols : q_cols + kv_cols],
        qkv_grad[:, q_cols + kv_cols :],
        out_proj_grad,
        gate_grad,
        up_grad,
        down_grad,
        gain_grads[0],
        gain_grads[1],
    )


def solution(mesh):
    rows, both = P("dp", None), P("dp", "tensor")
    in_specs = (rows, P("dp"), P("dp"), *[both] * 7, P("dp"), P("dp"), rows)
    out_specs = (rows, rows, *[both] * 7, P("dp"), P("dp"))
    return jax.shard_map(
        on_device, mesh=mesh, in_specs=in_specs, out_specs=out_specs, check_vma=False
    )
```
